32 devices in a mesh: solver: 8 (over y, x, core), group: 4 (over z).
Axes of the slice: x: 2, y: 2, z: 4, core: 2. Of those that a mesh axis runs over, the one named last changes fastest.
Arguments:
- field: float32 [8, 8, 8, 8192], P(None, None, None, ('solver', 'group')), may hold values from -6 to 6
- first_weight: bfloat16 [8, 1024], replicated, may hold values from -2 to 2
- second_weight: bfloat16 [1024, 1], replicated, may hold values from -0.1875 to 0.1875
- face_edges: int32 [2, 256], replicated, may hold values from 0 to 63, as said below
- sample_index: int32 [2048], P(('solver', 'group')), may hold values from 0 to 31
- route: int32 [2048, 1], P(('solver', 'group')), may hold values from 0 to 7; in each aligned block of 64 rows (0 to 63, 64 to 127, ...) at most 16 rows name the same one
Outputs:
- new_field: float32 [8, 8, 8, 8192], P(None, None, None, ('solver', 'group'))
- new_first: bfloat16 [8, 1024], replicated
- new_second: bfloat16 [1024, 1], replicated
The draws below stay inside these ranges and needn't reach their ends.
Inputs may be any that keep to these rules, and one draw needn't show every extreme that they name: `sample_index`: indices of wall elements (ey = 0) of the sample's own device, in the order ex * 8 + ez; they may repeat. `route`: at most 16 of the samples of one device name one learner, a bound that some block reaches by some device in every draw. `face_edges`: no edge joins a node to itself; edges may repeat.
All inputs are finite; a program needn't handle non-finite values.
Results may differ from the reference program's by a relative error of at most 0.001.
The reference program's roundings to bfloat16 on the way (of `features`) count: a program that leaves them out, or rounds other values in their place, can miss the bound.
Values sent between devices are 32-bit elements; how exact they have to be, the bound alone decides.
A program may use at most 128 MiB of HBM per device.

```python
import math
import jax
import jax.numpy as jnp
import numpy as np
from jax import lax

P_SIZE = 8
HID = 1024
EDGES = 256
FLOW_STEPS = 5
EXL = 4
EZL = 8
EY = 8
SAMPLES_DEV = 64
CAP = 16
ELEMS = 8192
N_SOLVER = 8
N_GROUP = 4


def draw_face_edges(key, part):
    first, second = jax.random.split(jax.random.fold_in(key, 11))
    source = jax.random.randint(first, (EDGES,), 0, P_SIZE * P_SIZE)
    offset = jax.random.randint(second, (EDGES,), 1, P_SIZE * P_SIZE)
    return jnp.stack([source, (source + offset) % (P_SIZE * P_SIZE)]).astype(jnp.int32)


def with_ends(values, rng, smallest, largest):
    index_at = [jax.random.randint(jax.random.fold_in(rng, axis), (), 0, length) for axis, length in enumerate(values.shape)]
    main_axis = values.shape.index(max(values.shape))
    next_to = index_at[:main_axis] + [(index_at[main_axis] + 1) % values.shape[main_axis]] + index_at[main_axis + 1:]
    return values.at[tuple(index_at)].set(smallest).at[tuple(next_to)].set(largest)


def block_scale(key, extent, shards, least, largest):
    def one(axis_at, shards_of):
        heights = jax.random.uniform(jax.random.fold_in(jax.random.fold_in(key, 6), axis_at), (shards_of,), jnp.float32, least / len(shards), largest / len(shards))
        return jnp.repeat(jnp.exp(heights), extent[axis_at] // shards_of).reshape((-1,) + (1,) * (len(extent) - axis_at - 1))

    factor_of = one(*shards[0])
    for cut in shards[1:]:
        factor_of = factor_of * one(*cut)
    return factor_of


def routed_block(own_key, own, number, rows, amount, top, most, lean):
    ranking = jax.random.permutation(own_key, amount)
    crowded, common = shares(amount, rows * top, most, lean, True), shares(amount, rows * top, most, lean, False)
    places = jnp.arange(amount)

    def named(lengths, turn):
        used = int((lengths > 0).sum())
        fixed = max(1, used // 4)
        shifted = fixed + (places - fixed + turn * (used - fixed)) % max(1, amount - fixed)
        return jnp.zeros((amount,), jnp.int32).at[ranking[jnp.where(places < fixed, places, shifted)]].set(jnp.asarray(lengths, jnp.int32))

    lengths = jnp.where(number % 4 == 0, named(crowded, number // 4), named(common, number - number // 4 - 1))
    mixed = jax.random.permutation(jax.random.fold_in(own, 3), amount)
    source_of, taker = mixed[0:amount // 2 * 2:2], mixed[1:amount // 2 * 2:2]
    slack = jnp.minimum(lengths[source_of] - 1, most - lengths[taker]) // 2
    slack = jnp.where((source_of == ranking[0]) | (taker == ranking[0]) | (lengths[taker] == 0), 0, jnp.maximum(slack, 0))
    shifted = jax.random.randint(jax.random.fold_in(own, 4), (amount // 2,), 0, 1 << 20) % (slack + 1)
    lengths = lengths.at[source_of].add(-shifted).at[taker].add(shifted)
    labels = jnp.searchsorted(jnp.cumsum(lengths), jnp.arange(rows * top), side="right").astype(jnp.int32)
    table = labels.reshape(top, rows).T
    table = table[jax.random.permutation(jax.random.fold_in(own, 1), rows)]
    turn = jax.random.randint(jax.random.fold_in(own, 2), (rows, 1), 0, top)
    return jnp.take_along_axis(table, (jnp.arange(top)[None, :] + turn) % top, axis=1)


def shares(amount, total, reach, lean, full):
    weights = [(1 << 20) // math.isqrt(standing ** lean) + 1 for standing in range(1, amount + 1)]
    largest = reach if full else min(reach, max(-(-total // amount), total * weights[0] // sum(weights)))
    least = 1 if total - largest >= amount - 1 else 0
    given, spare = [largest] + [least] * (amount - 1), total - largest - least * (amount - 1)
    while spare > 0:
        movable = [i for i in range(1, amount) if given[i] < largest] or [i for i in range(1, amount) if given[i] < reach]
        mass, remaining = sum([weights[i] for i in movable]), spare
        for i in movable:
            more = min(reach - given[i], max(1, remaining * weights[i] // mass), spare)
            given[i] = given[i] + more
            spare = spare - more
    return np.array(given)


def centred(key, extent, scale, bound, cuts=(), held_as=jnp.bfloat16):
    values = scale * jax.random.normal(key, extent, jnp.float32)
    if cuts:
        values = values * block_scale(key, extent, cuts, -0.22, 0.18)
    return jnp.clip(values, -bound, bound).astype(held_as)


def setup_inputs(seed: int = 0) -> dict:
    key_list = jax.random.split(jax.random.key(seed), 7)
    field = centred(key_list[0], (P_SIZE, P_SIZE, P_SIZE, ELEMS), 1.0, 6.0, ((3, 32),), jnp.float32)
    first_weight = centred(key_list[1], (P_SIZE, HID), P_SIZE ** -0.5, 2.0)
    second_weight = centred(key_list[2], (HID, 1), HID ** -0.5, 0.1875)
    face_edges = draw_face_edges(jax.random.fold_in(key_list[6], 71), 0)
    sample_index = with_ends(jax.random.randint(key_list[4], (N_SOLVER * N_GROUP * SAMPLES_DEV,), 0, EXL * EZL), jax.random.fold_in(key_list[4], 1), 0, (EXL * EZL) - 1).astype(jnp.int32)
    route_keys = jax.random.split(jax.random.fold_in(key_list[5], 1), (N_SOLVER * N_GROUP * SAMPLES_DEV) // SAMPLES_DEV)
    route_turns = jax.random.permutation(jax.random.fold_in(key_list[5], 3), (N_SOLVER * N_GROUP * SAMPLES_DEV) // SAMPLES_DEV)
    route = jax.vmap(lambda own, number: routed_block(jax.random.fold_in(key_list[5], 2), own, number, SAMPLES_DEV, N_SOLVER, 1, CAP, 2))(route_keys, route_turns).reshape((N_SOLVER * N_GROUP * SAMPLES_DEV, 1))
    return dict(field=field, first_weight=first_weight, second_weight=second_weight, face_edges=face_edges, sample_index=sample_index, route=route)


HIGH = lax.Precision.HIGHEST
TIME_STEP = 0.002
VISCOSITY = 0.01
VELOCITY = 1.0
PENALTY = 1.0
STRESS_SCALE = 0.1
LEARN_RATE = 0.05


def legendre_table(points_x, points):
    table = np.zeros((points_x.shape[0], points))
    table[:, 0] = 1.0
    table[:, 1] = points_x
    for degree in range(2, points):
        table[:, degree] = ((2 * degree - 1) * points_x * table[:, degree - 1] - (degree - 1) * table[:, degree - 2]) / degree
    return table


def gll_tables(points):
    order = points - 1
    guess = np.cos(np.pi * np.arange(points) / order)
    for sweep in range(100):
        table = legendre_table(guess, points)
        guess = guess - (guess * table[:, order] - table[:, order - 1]) / (points * table[:, order])
    nodes = guess[::-1]
    values = legendre_table(nodes, points)[:, order]
    matrix = np.zeros((points, points))
    for row in range(points):
        for column in range(points):
            if row != column:
                matrix[row, column] = values[row] / (values[column] * (nodes[row] - nodes[column]))
    matrix[0, 0] = -order * (order + 1) / 4.0
    matrix[order, order] = order * (order + 1) / 4.0
    return jnp.asarray(matrix, jnp.float32), 2.0 / (order * (order + 1))


def face_adjacency(face_edges, nodes):
    columns = jnp.arange(nodes, dtype=jnp.int32)
    source = (face_edges[0][:, None] == columns[None, :]).astype(jnp.float32)
    target = (face_edges[1][:, None] == columns[None, :]).astype(jnp.float32)
    single = jnp.dot(source.T, target, precision=HIGH)
    tile = 128 // nodes
    return (0.25 * jnp.kron(jnp.eye(tile, dtype=jnp.float32), single)).astype(jnp.bfloat16)


def network_output(first_weight, second_weight, adjacency, features):
    width = first_weight.shape[1]
    tile = adjacency.shape[0]
    inputs = jnp.transpose(features, (1, 0, 2)).reshape(features.shape[1], -1)
    before = jnp.dot(first_weight.T, inputs, preferred_element_type=jnp.float32)
    hidden = jnp.maximum(before, 0.0).astype(jnp.bfloat16)
    spread = jnp.einsum('hbn,nm->hbm', hidden.reshape(width, -1, tile).astype(jnp.float32), adjacency.astype(jnp.float32)).reshape(width, -1)
    mixed = (hidden.astype(jnp.float32) + spread).astype(jnp.bfloat16)
    output = jnp.dot(second_weight.T, mixed, preferred_element_type=jnp.float32)
    return inputs, before, mixed, output


def block_grads(first_weight, second_weight, adjacency, features, target, share):
    width = first_weight.shape[1]
    tile = adjacency.shape[0]
    inputs, before, mixed, output = network_output(first_weight, second_weight, adjacency, features)
    node_share = jnp.repeat(share, features.shape[2])[None, :]
    error = ((output - target.reshape(1, -1).astype(jnp.float32)) * node_share).astype(jnp.bfloat16)
    grad_second = lax.dot_general(mixed, error, (((1,), (1,)), ((), ())), preferred_element_type=jnp.float32)
    back_mixed = jnp.dot(second_weight, error, preferred_element_type=jnp.float32).astype(jnp.bfloat16)
    back_spread = jnp.einsum('hbm,nm->hbn', back_mixed.reshape(width, -1, tile).astype(jnp.float32), adjacency.astype(jnp.float32)).reshape(width, -1)
    back_hidden = jnp.where(before > 0.0, back_mixed.astype(jnp.float32) + back_spread, 0.0).astype(jnp.bfloat16)
    grad_first = lax.dot_general(inputs, back_hidden, (((1,), (1,)), ((), ())), preferred_element_type=jnp.float32)
    return grad_first, grad_second


def learner_grads(first_weight, second_weight, adjacency, features, target, share):
    group_size = 32
    blocks = features.shape[0] // group_size
    points = features.shape[1]
    face = features.shape[2]

    def one_block(carry, pieces):
        grads = block_grads(first_weight, second_weight, adjacency, pieces[0], pieces[1], pieces[2])
        return (carry[0] + grads[0], carry[1] + grads[1]), None

    start = (jnp.zeros(first_weight.shape, jnp.float32), jnp.zeros(second_weight.shape, jnp.float32))
    pieces = (features.reshape(blocks, group_size, points, face), target.reshape(blocks, group_size, face), share.reshape(blocks, group_size))
    result, unused = lax.scan(one_block, start, pieces)
    return result


def flow_step(field, stress, deriv, second_deriv, gain):
    points = field.shape[0]
    last = points - 1
    along_x = jnp.einsum('ai,ijkxzy->ajkxzy', deriv, field, precision=HIGH)
    curve = (jnp.einsum('ai,ijkxzy->ajkxzy', second_deriv, field, precision=HIGH)
             + jnp.einsum('aj,ijkxzy->iakxzy', second_deriv, field, precision=HIGH)
             + jnp.einsum('ak,ijkxzy->ijaxzy', second_deriv, field, precision=HIGH))
    change = -2.0 * VELOCITY * along_x + 4.0 * VISCOSITY * curve
    before_x = jnp.roll(field[last], 1, axis=2)
    after_x = jnp.roll(field[0], -1, axis=2)
    before_z = jnp.roll(field[:, :, last], 1, axis=3)
    after_z = jnp.roll(field[:, :, 0], -1, axis=3)
    lower = field[:, 0]
    upper = field[:, last]
    lower_jump = PENALTY * (upper[..., :-1] - lower[..., 1:])
    lower_term = jnp.concatenate([stress[..., None], lower_jump], axis=4)
    above = jnp.concatenate([lower[..., 1:], jnp.zeros_like(lower[..., :1])], axis=4)
    upper_term = PENALTY * (above - upper)
    change = change.at[0].add(gain * (VELOCITY + PENALTY) * (before_x - field[0]))
    change = change.at[last].add(gain * PENALTY * (after_x - field[last]))
    change = change.at[:, :, 0].add(gain * PENALTY * (before_z - field[:, :, 0]))
    change = change.at[:, :, last].add(gain * PENALTY * (after_z - field[:, :, last]))
    change = change.at[:, 0].add(gain * lower_term)
    change = change.at[:, last].add(gain * upper_term)
    return field + TIME_STEP * change


def reference(field, first_weight, second_weight, face_edges, sample_index, route):
    points = P_SIZE
    face = points * points
    deriv, end_weight = gll_tables(points)
    second_deriv = jnp.dot(deriv, deriv, precision=HIGH)
    gain = 2.0 / end_weight
    devices = N_SOLVER * N_GROUP
    walls = EXL * EZL
    adjacency = face_adjacency(face_edges, face)
    blocks = field.reshape(points, points, points, devices, EXL, EZL, EY)
    wall_field = blocks[..., 0].reshape(points, points, points, devices, walls)
    features = jnp.transpose(wall_field, (3, 4, 1, 0, 2)).reshape(devices, walls, points, face).astype(jnp.bfloat16)
    slope = jnp.einsum('j,ijkdw->dwik', deriv[0], wall_field, precision=HIGH)
    target = (STRESS_SCALE * slope).reshape(devices, walls, face).astype(jnp.bfloat16)
    index = sample_index.reshape(devices, SAMPLES_DEV)
    owners = jnp.arange(devices, dtype=jnp.int32)[:, None]
    sample_features = features[owners, index].reshape(-1, points, face)
    sample_target = target[owners, index].reshape(-1, face)
    destination = route[:, 0].reshape(N_SOLVER, N_GROUP, SAMPLES_DEV)
    learners = jnp.arange(N_SOLVER, dtype=jnp.int32)
    hits = (destination[..., None] == learners[None, None, None, :]).astype(jnp.float32)
    counts = jnp.sum(hits, axis=(0, 2))
    share = jnp.einsum('sgrl,gl->sgr', hits, 1.0 / (jnp.maximum(counts, 1.0) * devices), precision=HIGH).reshape(-1)
    grad_first, grad_second = learner_grads(first_weight, second_weight, adjacency, sample_features, sample_target, share)
    new_first = (first_weight.astype(jnp.float32) - LEARN_RATE * grad_first).astype(jnp.bfloat16)
    new_second = (second_weight.astype(jnp.float32) - LEARN_RATE * grad_second).astype(jnp.bfloat16)
    every_wall = features.reshape(-1, 32, points, face)

    def infer(block):
        return network_output(new_first, new_second, adjacency, block)[3]

    outputs = lax.map(infer, every_wall)
    stress = outputs.reshape(N_SOLVER, N_GROUP, EXL, EZL, points, points)
    stress = jnp.transpose(stress, (4, 5, 0, 2, 1, 3)).reshape(points, points, N_SOLVER * EXL, N_GROUP * EZL)
    grid = field.reshape(points, points, points, N_SOLVER, N_GROUP, EXL, EZL, EY)
    grid = jnp.transpose(grid, (0, 1, 2, 3, 5, 4, 6, 7)).reshape(points, points, points, N_SOLVER * EXL, N_GROUP * EZL, EY)
    for step in range(FLOW_STEPS):
        grid = flow_step(grid, stress, deriv, second_deriv, gain)
    grid = grid.reshape(points, points, points, N_SOLVER, EXL, N_GROUP, EZL, EY)
    new_field = jnp.transpose(grid, (0, 1, 2, 3, 5, 4, 6, 7)).reshape(points, points, points, -1)
    return new_field, new_first, new_second
```

```python
import jax
import jax.numpy as jnp
import numpy as np
from jax import lax
from jax.experimental import pallas as pl
from jax.experimental.pallas import tpu as pltpu
from jax.sharding import PartitionSpec as P

FLOW_STEPS = 5
EXL = 4
EZL = 8
EY = 8

HIGH = lax.Precision.HIGHEST
TIME_STEP = 0.002
VISCOSITY = 0.01
VELOCITY = 1.0
PENALTY = 1.0
STRESS_SCALE = 0.1
LEARN_RATE = 0.05
LANES = 128
F32 = jnp.float32
BF16 = jnp.bfloat16


def legendre_table(points_x, points):
    table = np.zeros((points_x.shape[0], points))
    table[:, 0] = 1.0
    table[:, 1] = points_x
    for degree in range(2, points):
        table[:, degree] = (
            (2 * degree - 1) * points_x * table[:, degree - 1] - (degree - 1) * table[:, degree - 2]
        ) / degree
    return table


def gll_tables(points):
    order = points - 1
    guess = np.cos(np.pi * np.arange(points) / order)
    for sweep in range(100):
        table = legendre_table(guess, points)
        guess = guess - (guess * table[:, order] - table[:, order - 1]) / (points * table[:, order])
    nodes = guess[::-1]
    values = legendre_table(nodes, points)[:, order]
    matrix = np.zeros((points, points))
    for row in range(points):
        for column in range(points):
            if row != column:
                matrix[row, column] = values[row] / (values[column] * (nodes[row] - nodes[column]))
    matrix[0, 0] = -order * (order + 1) / 4.0
    matrix[order, order] = order * (order + 1) / 4.0
    return matrix.astype(np.float32), 2.0 / (order * (order + 1))


def element_operator(deriv, gain):
    points = deriv.shape[0]
    last = points - 1
    deriv = deriv.astype(np.float64)
    second = 4.0 * VISCOSITY * (deriv @ deriv)
    along_i = -2.0 * VELOCITY * deriv + second
    along_i[0, 0] -= gain * (VELOCITY + PENALTY)
    along_i[last, last] -= gain * PENALTY
    other = second.copy()
    other[0, 0] -= gain * PENALTY
    other[last, last] -= gain * PENALTY
    eye = np.eye(points)
    whole = (
        np.kron(np.kron(along_i, eye), eye)
        + np.kron(np.kron(eye, other), eye)
        + np.kron(np.kron(eye, eye), other)
    )
    whole = (TIME_STEP * whole).astype(np.float32)
    high = whole.astype(jnp.bfloat16)
    low = (whole - high.astype(np.float32)).astype(jnp.bfloat16)
    return high, low


def make_kernel(learners, groups, points, width, deriv, gain):
    face = points * points
    last = points - 1
    nodes = face * points
    walls = EXL * EZL
    elements = walls * EY
    per_tile = LANES // walls
    tiles = face // per_tile
    pairs = tiles // 2
    owners = min(learners, width // LANES)
    owned = width // owners
    devices = learners * groups
    block = EZL * EY
    half = LANES // 2
    step_gain = float(TIME_STEP * gain * PENALTY)
    step_gain_x = float(TIME_STEP * gain * (VELOCITY + PENALTY))
    first_row = [float(value) for value in deriv[0]]

    def roll(value, shift):
        shift = shift % LANES
        return value if shift == 0 else pltpu.roll(value, shift, 1)

    def kernel(
        field_ref, first_ref, second_ref, edges_ref, index_ref, route_ref, high_ref, low_ref,
        out_ref, new_first_ref, new_second_ref,
        u_ref, v_ref, mask_ref, feat_ref, z_ref, grow_ref, w2_ref, acc_ref,
        count_ref, tile_ref, part_ref, cross_ref, total_ref, stress_ref,
        xs_ref, xr_ref, zs_ref, zr_ref,
        count_send, count_recv, part_send, part_recv, cross_send, cross_recv,
        total_send, total_recv, xs_send, xr_recv, zs_send, zr_recv,
    ):
        me = lax.axis_index("solver")
        mine = lax.axis_index("group")

        def peer_s(offset):
            return lax.rem(me + offset, learners)

        def peer_g(offset):
            return lax.rem(mine + offset, groups)

        barrier = pltpu.get_barrier_semaphore()
        for offset in range(1, learners):
            pl.semaphore_signal(
                barrier, inc=1, device_id={"solver": peer_s(offset)},
                device_id_type=pl.DeviceIdType.MESH,
            )
        for offset in range(1, groups):
            pl.semaphore_signal(
                barrier, inc=1, device_id={"group": peer_g(offset)},
                device_id_type=pl.DeviceIdType.MESH,
            )

        def remote(source, target, send, recv, where):
            return pltpu.make_async_remote_copy(
                src_ref=source, dst_ref=target, send_sem=send, recv_sem=recv,
                device_id=where, device_id_type=pl.DeviceIdType.MESH,
            )

        lane = lax.broadcasted_iota(jnp.int32, (1, LANES), 1)
        low_half = lane < half
        slot = lax.rem(lane, block) // EY
        level = lax.rem(lane, EY)

        learner_rows = lax.broadcasted_iota(jnp.int32, (learners, route_ref.shape[1]), 0)
        hits = (route_ref[...] == learner_rows).astype(F32)
        count_ref[me] = jnp.broadcast_to(jnp.sum(hits, axis=1, keepdims=True), (learners, LANES))

        def copies(step):
            right, left = {"solver": peer_s(1)}, {"solver": peer_s(learners - 1)}
            up, down = {"group": peer_g(1)}, {"group": peer_g(groups - 1)}
            result = []
            for side, where in ((0, right), (1, left)):
                result.append(remote(
                    xs_ref.at[step, side], xr_ref.at[step, side],
                    xs_send.at[step, side], xr_recv.at[step, side], where))
            for side, where in ((0, up), (1, down)):
                result.append(remote(
                    zs_ref.at[step, side], zr_ref.at[step, side],
                    zs_send.at[step, side], zr_recv.at[step, side], where))
            return result

        half_face = face // 2

        def send_faces(step):
            upper = u_ref[1, pl.ds(nodes - face, face), :]
            xs_ref[step, 0] = jnp.where(low_half, roll(upper[:half_face], half), upper[half_face:])
            lower = u_ref[0, pl.ds(0, face), :]
            xs_ref[step, 1] = jnp.where(low_half, lower[:half_face], roll(lower[half_face:], half))
            for part in range(2):
                high_pack = jnp.zeros((points, LANES), F32)
                low_pack = jnp.zeros((points, LANES), F32)
                for i in range(points):
                    top = u_ref[part, pl.ds(i * face + last, points, stride=points), :]
                    high_pack = jnp.where(slot == i, roll(top, EY * (i + 1)), high_pack)
                    bottom = u_ref[part, pl.ds(i * face, points, stride=points), :]
                    low_pack = jnp.where(slot == i, roll(bottom, EY * i), low_pack)
                zs_ref[step, 0, part] = high_pack
                zs_ref[step, 1, part] = low_pack
            for copy in copies(step):
                copy.start()

        for part in range(2):
            u_ref[part] = field_ref[:, part * LANES:(part + 1) * LANES]
        pl.semaphore_wait(barrier, learners + groups - 2)
        for offset in range(1, learners):
            remote(count_ref.at[me], count_ref.at[me], count_send.at[offset], count_recv.at[me],
                   {"solver": peer_s(offset)}).start()
        send_faces(0)

        rows = lax.broadcasted_iota(jnp.int32, (elements, LANES), 0)
        cols = lax.broadcasted_iota(jnp.int32, (elements, LANES), 1)
        picked = jnp.zeros((tiles * points, LANES), F32)
        first_select = None
        for q in range(per_tile):
            local = cols - q * walls
            select = ((rows == local * EY) & (local >= 0) & (local < walls)).astype(F32).astype(BF16)
            if q == 0:
                first_select = select
            pieces = []
            for m in range(tiles):
                node = m * per_tile + q
                start = (node // points) * face + node % points
                pieces.append(jnp.concatenate(
                    [u_ref[part, pl.ds(start, points, stride=points), :] for part in range(2)],
                    axis=1))
            stacked = jnp.concatenate(pieces, axis=0).astype(BF16)
            picked = picked + jnp.dot(stacked, select, preferred_element_type=F32)
        for m in range(tiles):
            feat_ref[m // 2, :, pl.ds((m % 2) * LANES, LANES)] = picked[m * points:(m + 1) * points]
        slopes = []
        for i in range(points):
            total = None
            for j in range(points):
                term = first_row[j] * field_ref[pl.ds(i * face + j * points, points), :]
                total = term if total is None else total + term
            slopes.append(STRESS_SCALE * total)
        target = jnp.dot(
            jnp.concatenate(slopes, axis=0).astype(BF16), first_select, preferred_element_type=F32
        )

        edge_rows = lax.broadcasted_iota(jnp.int32, (face, edges_ref.shape[1]), 0)
        tile_rows = lax.rem(edge_rows, tiles) * per_tile + edge_rows // tiles
        source = (edges_ref[0:1, :] == tile_rows).astype(F32).astype(BF16)
        sink = (edges_ref[1:2, :] == edge_rows).astype(F32).astype(BF16)
        contract = (((1,), (1,)), ((), ()))
        node_rows = lax.broadcasted_iota(jnp.int32, (face, face), 0)
        node_cols = lax.broadcasted_iota(jnp.int32, (face, face), 1)
        tile_node_rows = lax.rem(node_rows, tiles) * per_tile + node_rows // tiles
        tile_node_cols = lax.rem(node_cols, tiles) * per_tile + node_cols // tiles
        backward = 0.25 * lax.dot_general(source, sink, contract, preferred_element_type=F32)
        backward = backward + (tile_node_rows == node_cols).astype(F32)
        forward = 0.25 * lax.dot_general(sink, source, contract, preferred_element_type=F32)
        forward = forward + (node_rows == tile_node_cols).astype(F32)

        def network(first, second, keep_mask):
            turned = jnp.transpose(first).astype(BF16)
            w2_ref[...] = jnp.transpose(jnp.broadcast_to(second, (LANES, width)))

            def one(pair, carry):
                before = jnp.dot(turned, feat_ref[pair].astype(BF16), preferred_element_type=F32)
                if keep_mask:
                    mask_ref[pair] = jnp.where(before > 0.0, 1.0, 0.0).astype(BF16)
                hidden = jnp.maximum(before, 0.0)
                weight = w2_ref[...]
                z_ref[pl.ds(2 * pair, 1), :] = jnp.sum(
                    hidden[:, :LANES] * weight, axis=0, keepdims=True)
                z_ref[pl.ds(2 * pair + 1, 1), :] = jnp.sum(
                    hidden[:, LANES:] * weight, axis=0, keepdims=True)
                return carry

            lax.fori_loop(0, pairs, one, 0)
            z = z_ref[...]
            stacked = jnp.concatenate([roll(z, -walls * q) for q in range(per_tile)], axis=0)
            return jnp.dot(forward, stacked, precision=HIGH, preferred_element_type=F32)

        first = first_ref[...].astype(F32)
        second = second_ref[...].astype(F32)
        output = network(first, second, True)

        for offset in range(1, learners):
            origin = peer_s(offset)
            remote(count_ref.at[me], count_ref.at[origin], count_send.at[offset],
                   count_recv.at[origin], {"solver": origin}).wait_recv()
        counts = count_ref[0]
        for other in range(1, learners):
            counts = counts + count_ref[other]
        inverse = 1.0 / (jnp.maximum(counts[:, 0:1], 1.0) * devices)
        share = jnp.sum(hits * inverse, axis=0, keepdims=True)
        places = lax.broadcasted_iota(jnp.int32, (LANES, index_ref.shape[1]), 0)
        chosen = (index_ref[...] == places).astype(F32)
        weight = lax.dot_general(
            jnp.broadcast_to(share, (8, share.shape[1])), chosen, contract,
            precision=HIGH, preferred_element_type=F32,
        )[0:1]

        error = ((output - target) * weight).astype(BF16).astype(F32)
        g = jnp.dot(backward, error, precision=HIGH, preferred_element_type=F32)
        spread = g[0:tiles]
        for q in range(1, per_tile):
            spread = spread + roll(g[q * tiles:(q + 1) * tiles], walls * q)
        grow_ref[...] = spread
        acc_ref[...] = jnp.zeros_like(acc_ref)

        def back(pair, carry):
            scale = jnp.concatenate(
                [grow_ref[pl.ds(2 * pair, 1), :], grow_ref[pl.ds(2 * pair + 1, 1), :]], axis=1)
            scaled = feat_ref[pair] * scale
            upper = scaled.astype(BF16).astype(F32)
            both = jnp.concatenate([upper, scaled - upper], axis=0).astype(BF16)
            acc_ref[...] += lax.dot_general(
                both, mask_ref[pair], contract, preferred_element_type=F32)
            return carry

        lax.fori_loop(0, pairs, back, 0)
        grad = acc_ref[0:points, :] + acc_ref[points:2 * points, :]
        for t in range(owners):
            tile_ref[t] = grad[:, t * owned:(t + 1) * owned]

        def when_owner(which, action):
            if owners == learners:
                action()
            else:
                pl.when(which < owners)(action)

        def part_copy(offset):
            where = peer_s(offset)
            at = where if owners == learners else jnp.minimum(where, owners - 1)
            return where, remote(tile_ref.at[at], part_ref.at[me], part_send.at[offset],
                                 part_recv.at[me], {"solver": where})

        for offset in range(1, learners):
            where, copy = part_copy(offset)
            when_owner(where, copy.start)

        def reduce_owned():
            total = tile_ref[me if owners == learners else jnp.minimum(me, owners - 1)]
            for offset in range(1, learners):
                origin = peer_s(offset)
                remote(tile_ref.at[0], part_ref.at[origin], part_send.at[offset],
                       part_recv.at[origin], {"solver": origin}).wait_recv()
            for offset in range(1, learners):
                total = total + part_ref[peer_s(offset)]
            cross_ref[mine] = total
            for offset in range(1, groups):
                remote(cross_ref.at[mine], cross_ref.at[mine], cross_send.at[offset],
                       cross_recv.at[mine], {"group": peer_g(offset)}).start()
            for offset in range(1, groups):
                origin = peer_g(offset)
                remote(cross_ref.at[mine], cross_ref.at[origin], cross_send.at[offset],
                       cross_recv.at[origin], {"group": origin}).wait_recv()
            total = cross_ref[0]
            for other in range(1, groups):
                total = total + cross_ref[other]
            total_ref[me if owners == learners else jnp.minimum(me, owners - 1)] = total
            at = me if owners == learners else jnp.minimum(me, owners - 1)
            for offset in range(1, learners):
                remote(total_ref.at[at], total_ref.at[at], total_send.at[offset],
                       total_recv.at[at], {"solver": peer_s(offset)}).start()

        when_owner(me, reduce_owned)
        for offset in range(1, learners):
            origin = peer_s(offset)
            at = origin if owners == learners else jnp.minimum(origin, owners - 1)
            copy = remote(total_ref.at[at], total_ref.at[at], total_send.at[offset],
                          total_recv.at[at], {"solver": origin})
            when_owner(origin, copy.wait_recv)

        grad = jnp.concatenate([total_ref[t] for t in range(owners)], axis=1)
        new_first = (first - LEARN_RATE * (grad * second)).astype(BF16)
        grad_second = jnp.sum(first * grad, axis=0, keepdims=True)
        new_second = (second - LEARN_RATE * grad_second).astype(BF16)
        new_first_ref[...] = new_first
        new_second_ref[...] = new_second

        output = network(new_first.astype(F32), new_second.astype(F32), False)
        rows_t = lax.broadcasted_iota(jnp.int32, (LANES, elements), 0)
        cols_t = lax.broadcasted_iota(jnp.int32, (LANES, elements), 1)
        place = ((cols_t == rows_t * EY) & (rows_t < walls)).astype(F32)
        stress_ref[...] = jnp.dot(output, place, precision=HIGH, preferred_element_type=F32)

        def flow(step, carry):
            u = jnp.concatenate([u_ref[0], u_ref[1]], axis=1)
            upper = u.astype(BF16)
            lower = (u - upper.astype(F32)).astype(BF16)
            change = (
                jnp.dot(high_ref[...], upper, preferred_element_type=F32)
                + jnp.dot(high_ref[...], lower, preferred_element_type=F32)
                + jnp.dot(low_ref[...], upper, preferred_element_type=F32)
            )
            u = u + change
            for part in range(2):
                v_ref[part] = u[:, part * LANES:(part + 1) * LANES]
            for part in range(2):
                columns = pl.ds(part * LANES, LANES)
                for i in range(points):
                    base = i * face
                    bottom = u_ref[part, pl.ds(base, points), :]
                    top = u_ref[part, pl.ds(base + face - points, points), :]
                    stress = stress_ref[pl.ds(i * points, points), columns]
                    below = jnp.where(level == 0, bottom + stress, roll(top, 1))
                    above = jnp.where(level == EY - 1, 0.0, roll(bottom, -1))
                    v_ref[part, pl.ds(base, points), :] += step_gain * below
                    v_ref[part, pl.ds(base + face - points, points), :] += step_gain * above
            for copy in copies(step):
                copy.wait_recv()
            low0 = roll(u_ref[0, pl.ds(nodes - face, face), :], half)
            low1 = roll(u_ref[1, pl.ds(nodes - face, face), :], half)
            halo = xr_ref[step, 0]
            halo = jnp.concatenate([halo, roll(halo, half)], axis=0)
            v_ref[0, pl.ds(0, face), :] += step_gain_x * jnp.where(low_half, halo, low0)
            v_ref[1, pl.ds(0, face), :] += step_gain_x * jnp.where(low_half, low0, low1)
            high0 = roll(u_ref[0, pl.ds(0, face), :], half)
            high1 = roll(u_ref[1, pl.ds(0, face), :], half)
            halo = xr_ref[step, 1]
            halo = jnp.concatenate([roll(halo, half), halo], axis=0)
            v_ref[0, pl.ds(nodes - face, face), :] += step_gain * jnp.where(
                low_half, high0, high1)
            v_ref[1, pl.ds(nodes - face, face), :] += step_gain * jnp.where(
                low_half, high1, halo)
            for part in range(2):
                before_pack = zr_ref[step, 0, part]
                after_pack = zr_ref[step, 1, part]
                for i in range(points):
                    near = pl.ds(i * face, points, stride=points)
                    far = pl.ds(i * face + last, points, stride=points)
                    top = u_ref[part, far, :]
                    bottom = u_ref[part, near, :]
                    before = jnp.where(slot == 0, roll(before_pack, half - EY * i), roll(top, EY))
                    after = jnp.where(
                        slot == EZL - 1, roll(after_pack, EY * (EZL - 1 - i)), roll(bottom, -EY))
                    v_ref[part, near, :] = v_ref[part, near, :] + step_gain * before
                    v_ref[part, far, :] = v_ref[part, far, :] + step_gain * after
            u_ref[...] = v_ref[...]

            @pl.when(step < FLOW_STEPS - 1)
            def _():
                send_faces(step + 1)

            return carry

        lax.fori_loop(0, FLOW_STEPS, flow, 0)
        for part in range(2):
            out_ref[:, part * LANES:(part + 1) * LANES] = v_ref[part]

        for offset in range(1, learners):
            remote(count_ref.at[me], count_ref.at[me], count_send.at[offset], count_recv.at[me],
                   {"solver": peer_s(offset)}).wait_send()
            where, copy = part_copy(offset)
            when_owner(where, copy.wait_send)

        def drain_owned():
            at = me if owners == learners else jnp.minimum(me, owners - 1)
            for offset in range(1, groups):
                remote(cross_ref.at[mine], cross_ref.at[mine], cross_send.at[offset],
                       cross_recv.at[mine], {"group": peer_g(offset)}).wait_send()
            for offset in range(1, learners):
                remote(total_ref.at[at], total_ref.at[at], total_send.at[offset],
                       total_recv.at[at], {"solver": peer_s(offset)}).wait_send()

        when_owner(me, drain_owned)

        def drain(step, carry):
            for copy in copies(step):
                copy.wait_send()
            return carry

        lax.fori_loop(0, FLOW_STEPS, drain, 0)

    dma = pltpu.SemaphoreType.DMA
    scratch = [
        pltpu.VMEM((2, nodes, LANES), F32),
        pltpu.VMEM((2, nodes, LANES), F32),
        pltpu.VMEM((pairs, width, 2 * LANES), BF16),
        pltpu.VMEM((pairs, points, 2 * LANES), F32),
        pltpu.VMEM((tiles, LANES), F32),
        pltpu.VMEM((tiles, LANES), F32),
        pltpu.VMEM((width, LANES), F32),
        pltpu.VMEM((2 * points, width), F32),
        pltpu.VMEM((learners, learners, LANES), F32),
        pltpu.VMEM((owners, points, owned), F32),
        pltpu.VMEM((learners, points, owned), F32),
        pltpu.VMEM((groups, points, owned), F32),
        pltpu.VMEM((owners, points, owned), F32),
        pltpu.VMEM((face, elements), F32),
        pltpu.VMEM((FLOW_STEPS, 2, face // 2, LANES), F32),
        pltpu.VMEM((FLOW_STEPS, 2, face // 2, LANES), F32),
        pltpu.VMEM((FLOW_STEPS, 2, 2, points, LANES), F32),
        pltpu.VMEM((FLOW_STEPS, 2, 2, points, LANES), F32),
        dma((learners,)), dma((learners,)), dma((learners,)), dma((learners,)),
        dma((groups,)), dma((groups,)), dma((learners,)), dma((owners,)),
        dma((FLOW_STEPS, 2)), dma((FLOW_STEPS, 2)), dma((FLOW_STEPS, 2)), dma((FLOW_STEPS, 2)),
    ]
    return kernel, scratch


def shards(field, first_weight, second_weight, face_edges, sample_index, route):
    points = field.shape[0]
    elements = field.shape[3]
    nodes = points**3
    width = first_weight.shape[1]
    learners = lax.axis_size("solver")
    groups = lax.axis_size("group")
    deriv, end_weight = gll_tables(points)
    gain = 2.0 / end_weight
    high, low = element_operator(deriv, gain)
    kernel, scratch = make_kernel(learners, groups, points, width, deriv, gain)
    vmem = pl.BlockSpec(memory_space=pltpu.VMEM)
    new_field, new_first, new_second = pl.pallas_call(
        kernel,
        out_shape=(
            jax.ShapeDtypeStruct((nodes, elements), F32),
            jax.ShapeDtypeStruct(first_weight.shape, BF16),
            jax.ShapeDtypeStruct((1, width), BF16),
        ),
        in_specs=[vmem] * 8,
        out_specs=(vmem, vmem, vmem),
        scratch_shapes=scratch,
        compiler_params=pltpu.CompilerParams(
            collective_id=0, has_side_effects=True, vmem_limit_bytes=40 * 1024 * 1024
        ),
        name="step",
    )(
        field.reshape(nodes, elements),
        first_weight,
        second_weight.reshape(1, width),
        face_edges,
        sample_index.reshape(1, -1),
        route.reshape(1, -1),
        jnp.asarray(high),
        jnp.asarray(low),
    )
    return (new_field.reshape(field.shape), new_first, new_second.reshape(second_weight.shape))


def solution(mesh):
    return jax.shard_map(
        shards,
        mesh=mesh,
        in_specs=(
            P(None, None, None, ("solver", "group")),
            P(),
            P(),
            P(),
            P(("solver", "group")),
            P(("solver", "group"), None),
        ),
        out_specs=(P(None, None, None, ("solver", "group")), P(), P()),
        check_vma=False,
    )
```

```python
import jax
import jax.numpy as jnp
import numpy as np
from jax import lax
from jax.experimental import pallas as pl
from jax.experimental.pallas import tpu as pltpu
from jax.sharding import PartitionSpec as P

FLOW_STEPS = 5
EXL = 4
EZL = 8
EY = 8

HIGH = lax.Precision.HIGHEST
TIME_STEP = 0.002
VISCOSITY = 0.01
VELOCITY = 1.0
PENALTY = 1.0
STRESS_SCALE = 0.1
LEARN_RATE = 0.05
LANES = 128
F32 = jnp.float32
BF16 = jnp.bfloat16


def legendre_table(points_x, points):
    table = np.zeros((points_x.shape[0], points))
    table[:, 0] = 1.0
    table[:, 1] = points_x
    for degree in range(2, points):
        table[:, degree] = (
            (2 * degree - 1) * points_x * table[:, degree - 1] - (degree - 1) * table[:, degree - 2]
        ) / degree
    return table


def gll_tables(points):
    order = points - 1
    guess = np.cos(np.pi * np.arange(points) / order)
    for sweep in range(100):
        table = legendre_table(guess, points)
        guess = guess - (guess * table[:, order] - table[:, order - 1]) / (points * table[:, order])
    nodes = guess[::-1]
    values = legendre_table(nodes, points)[:, order]
    matrix = np.zeros((points, points))
    for row in range(points):
        for column in range(points):
            if row != column:
                matrix[row, column] = values[row] / (values[column] * (nodes[row] - nodes[column]))
    matrix[0, 0] = -order * (order + 1) / 4.0
    matrix[order, order] = order * (order + 1) / 4.0
    return matrix.astype(np.float32), 2.0 / (order * (order + 1))


def element_operator(deriv, gain):
    points = deriv.shape[0]
    last = points - 1
    deriv = deriv.astype(np.float64)
    second = 4.0 * VISCOSITY * (deriv @ deriv)
    along_i = -2.0 * VELOCITY * deriv + second
    along_i[0, 0] -= gain * (VELOCITY + PENALTY)
    along_i[last, last] -= gain * PENALTY
    other = second.copy()
    other[0, 0] -= gain * PENALTY
    other[last, last] -= gain * PENALTY
    eye = np.eye(points)
    whole = (
        np.kron(np.kron(along_i, eye), eye)
        + np.kron(np.kron(eye, other), eye)
        + np.kron(np.kron(eye, eye), other)
    )
    whole = (TIME_STEP * whole).astype(np.float32)
    high = whole.astype(jnp.bfloat16)
    low = (whole - high.astype(np.float32)).astype(jnp.bfloat16)
    return high, low


def make_kernel(learners, groups, points, width, deriv, gain):
    face = points * points
    last = points - 1
    nodes = face * points
    walls = EXL * EZL
    elements = walls * EY
    pairs = walls * face // (2 * LANES)
    owners = min(learners, width // LANES)
    owned = width // owners
    devices = learners * groups
    block = EZL * EY
    half = LANES // 2
    step_gain = float(TIME_STEP * gain * PENALTY)
    step_gain_x = float(TIME_STEP * gain * (VELOCITY + PENALTY))
    first_row = [float(value) for value in deriv[0]]

    def roll(value, shift):
        shift = shift % LANES
        return value if shift == 0 else pltpu.roll(value, shift, 1)

    rows_sent = points + 1
    lane_rows = walls * face // LANES

    def kernel(
        field_ref, first_ref, second_ref, edges_ref, index_ref, route_ref, high_hbm, low_hbm,
        out_ref, new_first_ref, new_second_ref,
        u_ref, high_ref, low_ref, mask_ref, mixed_ref, feat_ref, turn_ref, z_ref, g_ref, e_ref,
        w2_ref, acc_ref, acc2_ref,
        count_ref, tile_ref, part_ref, cross_ref, total_ref, stress_ref,
        xs_ref, xr_ref, zs_ref, zr_ref,
        load_sem, count_send, count_recv, part_send, part_recv, cross_send, cross_recv,
        total_send, total_recv, xs_send, xr_recv, zs_send, zr_recv,
    ):
        me = lax.axis_index("solver")
        mine = lax.axis_index("group")

        def peer_s(offset):
            return lax.rem(me + offset, learners)

        def peer_g(offset):
            return lax.rem(mine + offset, groups)

        loads = [
            pltpu.make_async_copy(
                field_ref.at[:, pl.ds(part * LANES, LANES)], u_ref.at[0, part], load_sem.at[part])
            for part in range(2)
        ]
        loads.append(pltpu.make_async_copy(high_hbm, high_ref, load_sem.at[2]))
        loads.append(pltpu.make_async_copy(low_hbm, low_ref, load_sem.at[3]))
        for load in loads:
            load.start()

        barrier = pltpu.get_barrier_semaphore()
        for offset in range(1, learners):
            pl.semaphore_signal(
                barrier, inc=1, device_id={"solver": peer_s(offset)},
                device_id_type=pl.DeviceIdType.MESH,
            )
        for offset in range(1, groups):
            pl.semaphore_signal(
                barrier, inc=1, device_id={"group": peer_g(offset)},
                device_id_type=pl.DeviceIdType.MESH,
            )

        def remote(source, target, send, recv, where):
            return pltpu.make_async_remote_copy(
                src_ref=source, dst_ref=target, send_sem=send, recv_sem=recv,
                device_id=where, device_id_type=pl.DeviceIdType.MESH,
            )

        lane = lax.broadcasted_iota(jnp.int32, (1, LANES), 1)
        low_half = lane < half
        slot = lax.rem(lane, block) // EY
        level = lax.rem(lane, EY)
        contract = (((1,), (1,)), ((), ()))

        learner_rows = lax.broadcasted_iota(jnp.int32, (learners, route_ref.shape[1]), 0)
        hits = (route_ref[...] == learner_rows).astype(F32)
        count_ref[me] = jnp.broadcast_to(jnp.sum(hits, axis=1, keepdims=True), (learners, LANES))

        big = 2 * LANES
        edge_rows = lax.rem(
            lax.broadcasted_iota(jnp.int32, (big, edges_ref.shape[1]), 0), face)
        source = (edges_ref[0:1, :] == edge_rows).astype(F32).astype(BF16)
        sink = (edges_ref[1:2, :] == edge_rows).astype(F32).astype(BF16)
        node_rows = lax.broadcasted_iota(jnp.int32, (big, big), 0)
        node_cols = lax.broadcasted_iota(jnp.int32, (big, big), 1)
        graph = 0.25 * lax.dot_general(source, sink, contract, preferred_element_type=F32)
        graph = jnp.where(node_rows // face == node_cols // face, graph, 0.0)
        graph = graph + (node_rows == node_cols).astype(F32)
        small = graph[:LANES, :LANES]
        graph = graph.astype(BF16)
        first = first_ref[...].astype(F32)
        second = second_ref[...].astype(F32)

        def copies(step):
            right, left = {"solver": peer_s(1)}, {"solver": peer_s(learners - 1)}
            up, down = {"group": peer_g(1)}, {"group": peer_g(groups - 1)}
            result = []
            for side, where in ((0, right), (1, left)):
                result.append(remote(
                    xs_ref.at[step, side], xr_ref.at[step, side],
                    xs_send.at[step, side], xr_recv.at[step, side], where))
            for side, where in ((0, up), (1, down)):
                result.append(remote(
                    zs_ref.at[step, side], zr_ref.at[step, side],
                    zs_send.at[step, side], zr_recv.at[step, side], where))
            return result

        half_face = face // 2

        def near(i):
            return pl.ds(i * face, points, stride=points)

        def far(i):
            return pl.ds(i * face + last, points, stride=points)

        def send_z(step, bottoms, tops):
            for part in range(2):
                high_pack = jnp.zeros((points, LANES), F32)
                low_pack = jnp.zeros((points, LANES), F32)
                for i in range(points):
                    high_pack = jnp.where(slot == i, roll(tops[part][i], EY * (i + 1)), high_pack)
                    low_pack = jnp.where(slot == i, roll(bottoms[part][i], EY * i), low_pack)
                zs_ref[step, 0, part] = high_pack
                zs_ref[step, 1, part] = low_pack
            every = copies(step)
            every[2].start()
            every[3].start()

        def send_x(step, u):
            upper = u[1, pl.ds(nodes - face, face), :]
            xs_ref[step, 0] = jnp.where(low_half, roll(upper[:half_face], half), upper[half_face:])
            lower = u[0, pl.ds(0, face), :]
            xs_ref[step, 1] = jnp.where(low_half, lower[:half_face], roll(lower[half_face:], half))
            every = copies(step)
            every[0].start()
            every[1].start()

        def send_faces(step, u):
            send_z(step, [[u[part, near(i), :] for i in range(points)] for part in range(2)],
                   [[u[part, far(i), :] for i in range(points)] for part in range(2)])
            send_x(step, u)

        start = u_ref.at[0]
        for load in loads[:2]:
            load.wait()

        def face_rows(value_of):
            rows = jnp.concatenate([value_of(i) for i in range(points)], axis=0)
            return jnp.concatenate([rows, rows], axis=0).astype(BF16)

        def plane(i, j):
            at = pl.ds(i * face + j * points, points)
            return jnp.concatenate([start[0, at, :], start[1, at, :]], axis=1)

        def slope(i):
            total = None
            for j in range(points):
                term = first_row[j] * plane(i, j)
                total = term if total is None else total + term
            return STRESS_SCALE * total

        wall_rows = lax.broadcasted_iota(jnp.int32, (walls, elements), 0)
        wall_cols = lax.broadcasted_iota(jnp.int32, (walls, elements), 1)
        select = (wall_cols == wall_rows * EY).astype(F32).astype(BF16)
        for j in range(points):
            turn_ref[pl.ds(j * walls, walls), :] = lax.dot_general(
                select, face_rows(lambda i: plane(i, j)), contract, preferred_element_type=F32)
        turn_ref[pl.ds(nodes // 2, walls), :] = lax.dot_general(
            select, face_rows(slope), contract, preferred_element_type=F32)
        for row in range(lane_rows):
            even = turn_ref[pl.ds(2 * row, points, stride=walls), :]
            odd = turn_ref[pl.ds(2 * row + 1, points, stride=walls), :]
            feat_ref[row // 2, :, pl.ds((row % 2) * LANES, LANES)] = jnp.where(low_half, even, odd)
        target = jnp.where(
            low_half,
            turn_ref[pl.ds(nodes // 2, lane_rows, stride=2), :],
            turn_ref[pl.ds(nodes // 2 + 1, lane_rows, stride=2), :],
        )

        pl.semaphore_wait(barrier, learners + groups - 2)
        for offset in range(1, learners):
            remote(count_ref.at[me], count_ref.at[me], count_send.at[offset], count_recv.at[me],
                   {"solver": peer_s(offset)}).start()
        send_faces(0, start)

        def network(first, second, learn):
            turned = jnp.transpose(first).astype(BF16)
            w2_ref[...] = jnp.transpose(jnp.broadcast_to(second, (LANES, width)))

            def one(pair, carry):
                before = jnp.dot(turned, feat_ref[pair].astype(BF16), preferred_element_type=F32)
                hidden = jnp.maximum(before, 0.0)
                if learn:
                    mask_ref[pair] = jnp.where(before > 0.0, 1.0, 0.0).astype(BF16)
                    mixed = jnp.dot(
                        hidden.astype(BF16), graph, preferred_element_type=F32).astype(BF16)
                    mixed_ref[pair] = mixed
                    hidden = mixed.astype(F32)
                weight = w2_ref[...]
                z_ref[pl.ds(2 * pair, 1), :] = jnp.sum(
                    hidden[:, :LANES] * weight, axis=0, keepdims=True)
                z_ref[pl.ds(2 * pair + 1, 1), :] = jnp.sum(
                    hidden[:, LANES:] * weight, axis=0, keepdims=True)
                return carry

            lax.fori_loop(0, pairs, one, 0)
            return z_ref[...]

        output = network(first, second, True)

        for offset in range(1, learners):
            origin = peer_s(offset)
            remote(count_ref.at[me], count_ref.at[origin], count_send.at[offset],
                   count_recv.at[origin], {"solver": origin}).wait_recv()
        counts = count_ref[0]
        for other in range(1, learners):
            counts = counts + count_ref[other]
        inverse = 1.0 / (jnp.maximum(counts, 1.0) * devices)
        places = 2 * lax.broadcasted_iota(jnp.int32, (lane_rows, index_ref.shape[1]), 0)
        chosen = (index_ref[...] == places).astype(F32)
        even = lax.dot_general(chosen, hits, contract, preferred_element_type=F32)
        chosen = (index_ref[...] == places + 1).astype(F32)
        odd = lax.dot_general(chosen, hits, contract, preferred_element_type=F32)
        difference = output - target
        error = jnp.zeros((lane_rows, LANES), F32)
        for learner in range(learners):
            times = jnp.where(low_half, even[:, learner:learner + 1], odd[:, learner:learner + 1])
            single = (difference * inverse[learner:learner + 1]).astype(BF16).astype(F32)
            error = error + times * single
        e_ref[...] = error
        g_ref[...] = lax.dot_general(
            error, small, contract, precision=HIGH, preferred_element_type=F32)

        acc_ref[...] = jnp.zeros_like(acc_ref)
        acc2_ref[...] = jnp.zeros_like(acc2_ref)

        def split(value):
            upper = value.astype(BF16).astype(F32)
            return jnp.concatenate([upper, value - upper], axis=0).astype(BF16)

        def row_pair(ref, pair):
            return jnp.concatenate([ref[pl.ds(2 * pair, 1), :], ref[pl.ds(2 * pair + 1, 1), :]], axis=1)

        def back(pair, carry):
            acc_ref[...] += lax.dot_general(
                split(feat_ref[pair] * row_pair(g_ref, pair)), mask_ref[pair], contract,
                preferred_element_type=F32)
            wide = jnp.broadcast_to(row_pair(e_ref, pair), (8, big))
            acc2_ref[...] += lax.dot_general(
                split(wide), mixed_ref[pair], contract, preferred_element_type=F32)
            return carry

        lax.fori_loop(0, pairs, back, 0)
        grad = acc_ref[0:points, :] + acc_ref[points:2 * points, :]
        grad_second = acc2_ref[0:1, :] + acc2_ref[8:9, :]
        for t in range(owners):
            tile_ref[t, pl.ds(0, points), :] = grad[:, t * owned:(t + 1) * owned]
            tile_ref[t, pl.ds(points, 1), :] = grad_second[:, t * owned:(t + 1) * owned]

        def when_owner(which, action):
            if owners == learners:
                action()
            else:
                pl.when(which < owners)(action)

        def clamp(which):
            return which if owners == learners else jnp.minimum(which, owners - 1)

        def part_copy(offset):
            where = peer_s(offset)
            return where, remote(tile_ref.at[clamp(where)], part_ref.at[me], part_send.at[offset],
                                 part_recv.at[me], {"solver": where})

        for offset in range(1, learners):
            where, copy = part_copy(offset)
            when_owner(where, copy.start)

        def local(source, target, stress):
            u = jnp.concatenate([source[0], source[1]], axis=1)
            upper = u.astype(BF16)
            lower = (u - upper.astype(F32)).astype(BF16)
            u = u + (
                jnp.dot(high_ref[...], upper, preferred_element_type=F32)
                + jnp.dot(high_ref[...], lower, preferred_element_type=F32)
                + jnp.dot(low_ref[...], upper, preferred_element_type=F32)
            )
            for part in range(2):
                target[part] = u[:, part * LANES:(part + 1) * LANES]
            for part in range(2):
                for i in range(points):
                    base = i * face
                    bottom = source[part, pl.ds(base, points), :]
                    top = source[part, pl.ds(base + face - points, points), :]
                    below = jnp.where(level == 0, bottom, roll(top, 1))
                    if stress:
                        below = below + stress_ref[part, pl.ds(i * points, points), :]
                    above = jnp.where(level == EY - 1, 0.0, roll(bottom, -1))
                    target[part, pl.ds(base, points), :] += step_gain * below
                    target[part, pl.ds(base + face - points, points), :] += step_gain * above
            low0 = roll(source[0, pl.ds(nodes - face, face), :], half)
            low1 = roll(source[1, pl.ds(nodes - face, face), :], half)
            target[0, pl.ds(0, face), :] += step_gain_x * jnp.where(low_half, 0.0, low0)
            target[1, pl.ds(0, face), :] += step_gain_x * jnp.where(low_half, low0, low1)
            high0 = roll(source[0, pl.ds(0, face), :], half)
            high1 = roll(source[1, pl.ds(0, face), :], half)
            target[0, pl.ds(nodes - face, face), :] += step_gain * jnp.where(low_half, high0, high1)
            target[1, pl.ds(nodes - face, face), :] += step_gain * jnp.where(low_half, high1, 0.0)
            for part in range(2):
                for i in range(points):
                    before = jnp.where(slot == 0, 0.0, roll(source[part, far(i), :], EY))
                    after = jnp.where(slot == EZL - 1, 0.0, roll(source[part, near(i), :], -EY))
                    target[part, near(i), :] = target[part, near(i), :] + step_gain * before
                    target[part, far(i), :] = target[part, far(i), :] + step_gain * after

        def halo(step, target, send):
            every = copies(step)
            every[0].wait_recv()
            every[1].wait_recv()
            ghost = xr_ref[step, 0]
            ghost = jnp.concatenate([ghost, roll(ghost, half)], axis=0)
            target[0, pl.ds(0, face), :] += step_gain_x * jnp.where(low_half, ghost, 0.0)
            ghost = xr_ref[step, 1]
            ghost = jnp.concatenate([roll(ghost, half), ghost], axis=0)
            target[1, pl.ds(nodes - face, face), :] += step_gain * jnp.where(low_half, 0.0, ghost)
            every[2].wait_recv()
            every[3].wait_recv()
            bottoms, tops = [], []
            for part in range(2):
                before_pack = step_gain * zr_ref[step, 0, part]
                after_pack = step_gain * zr_ref[step, 1, part]
                for i in range(points):
                    before = jnp.where(slot == 0, roll(before_pack, half - EY * i), 0.0)
                    after = jnp.where(
                        slot == EZL - 1, roll(after_pack, EY * (EZL - 1 - i)), 0.0)
                    bottoms.append(target[part, near(i), :] + before)
                    tops.append(target[part, far(i), :] + after)
                    target[part, near(i), :] = bottoms[-1]
                    target[part, far(i), :] = tops[-1]
            if send:
                send_z(step + 1, [bottoms[:points], bottoms[points:]], [tops[:points], tops[points:]])
                send_x(step + 1, target)

        for load in loads[2:]:
            load.wait()
        other = u_ref.at[1]
        local(start, other, False)
        halo(0, other, False)

        def reduce_owned():
            total = tile_ref[clamp(me)]
            for offset in range(1, learners):
                origin = peer_s(offset)
                remote(tile_ref.at[0], part_ref.at[origin], part_send.at[offset],
                       part_recv.at[origin], {"solver": origin}).wait_recv()
            for offset in range(1, learners):
                total = total + part_ref[peer_s(offset)]
            cross_ref[mine] = total
            for offset in range(1, groups):
                remote(cross_ref.at[mine], cross_ref.at[mine], cross_send.at[offset],
                       cross_recv.at[mine], {"group": peer_g(offset)}).start()
            for offset in range(1, groups):
                origin = peer_g(offset)
                remote(cross_ref.at[mine], cross_ref.at[origin], cross_send.at[offset],
                       cross_recv.at[origin], {"group": origin}).wait_recv()
            total = cross_ref[0]
            for origin in range(1, groups):
                total = total + cross_ref[origin]
            at = clamp(me)
            total_ref[at] = total
            for offset in range(1, learners):
                remote(total_ref.at[at], total_ref.at[at], total_send.at[offset],
                       total_recv.at[at], {"solver": peer_s(offset)}).start()

        when_owner(me, reduce_owned)
        for offset in range(1, learners):
            origin = peer_s(offset)
            at = clamp(origin)
            copy = remote(total_ref.at[at], total_ref.at[at], total_send.at[offset],
                          total_recv.at[at], {"solver": origin})
            when_owner(origin, copy.wait_recv)

        sums = jnp.concatenate([total_ref[t] for t in range(owners)], axis=1)
        grad = sums[0:points]
        new_first = (first - LEARN_RATE * (grad * second)).astype(BF16)
        new_second = (second - LEARN_RATE * sums[points:points + 1]).astype(BF16)
        new_first_ref[...] = new_first
        new_second_ref[...] = new_second

        plain = network(new_first.astype(F32), new_second.astype(F32), False)
        stress = jnp.dot(plain, small, precision=HIGH, preferred_element_type=F32)
        stress = jnp.transpose(stress)
        rows_t = 2 * lax.broadcasted_iota(jnp.int32, (lane_rows, elements), 0)
        cols_t = lax.broadcasted_iota(jnp.int32, (lane_rows, elements), 1)
        placed = jnp.dot(
            stress[:face], (cols_t == rows_t * EY).astype(F32),
            precision=HIGH, preferred_element_type=F32,
        ) + jnp.dot(
            stress[face:], (cols_t == (rows_t + 1) * EY).astype(F32),
            precision=HIGH, preferred_element_type=F32,
        )
        for part in range(2):
            columns = placed[:, part * LANES:(part + 1) * LANES]
            stress_ref[part] = columns
            for i in range(points):
                other[part, pl.ds(i * face, points), :] += (
                    step_gain * columns[i * points:(i + 1) * points])

        if FLOW_STEPS > 1:
            send_faces(1, other)
        held = [start, other]
        for step in range(1, FLOW_STEPS):
            final = step == FLOW_STEPS - 1
            source, target = held[step % 2], out_ref if final else held[(step + 1) % 2]
            local(source, target, True)
            halo(step, target, not final)

        for offset in range(1, learners):
            remote(count_ref.at[me], count_ref.at[me], count_send.at[offset], count_recv.at[me],
                   {"solver": peer_s(offset)}).wait_send()
            where, copy = part_copy(offset)
            when_owner(where, copy.wait_send)

        def drain_owned():
            at = clamp(me)
            for offset in range(1, groups):
                remote(cross_ref.at[mine], cross_ref.at[mine], cross_send.at[offset],
                       cross_recv.at[mine], {"group": peer_g(offset)}).wait_send()
            for offset in range(1, learners):
                remote(total_ref.at[at], total_ref.at[at], total_send.at[offset],
                       total_recv.at[at], {"solver": peer_s(offset)}).wait_send()

        when_owner(me, drain_owned)
        for step in range(FLOW_STEPS):
            for copy in copies(step):
                copy.wait_send()

    dma = pltpu.SemaphoreType.DMA
    scratch = [
        pltpu.VMEM((2, 2, nodes, LANES), F32),
        pltpu.VMEM((nodes, nodes), BF16),
        pltpu.VMEM((nodes, nodes), BF16),
        pltpu.VMEM((pairs, width, 2 * LANES), BF16),
        pltpu.VMEM((pairs, width, 2 * LANES), BF16),
        pltpu.VMEM((pairs, points, 2 * LANES), F32),
        pltpu.VMEM((nodes // 2 + walls, LANES), F32),
        pltpu.VMEM((lane_rows, LANES), F32),
        pltpu.VMEM((lane_rows, LANES), F32),
        pltpu.VMEM((lane_rows, LANES), F32),
        pltpu.VMEM((width, LANES), F32),
        pltpu.VMEM((2 * points, width), F32),
        pltpu.VMEM((16, width), F32),
        pltpu.VMEM((learners, learners, LANES), F32),
        pltpu.VMEM((owners, rows_sent, owned), F32),
        pltpu.VMEM((learners, rows_sent, owned), F32),
        pltpu.VMEM((groups, rows_sent, owned), F32),
        pltpu.VMEM((owners, rows_sent, owned), F32),
        pltpu.VMEM((2, face, LANES), F32),
        pltpu.VMEM((FLOW_STEPS, 2, face // 2, LANES), F32),
        pltpu.VMEM((FLOW_STEPS, 2, face // 2, LANES), F32),
        pltpu.VMEM((FLOW_STEPS, 2, 2, points, LANES), F32),
        pltpu.VMEM((FLOW_STEPS, 2, 2, points, LANES), F32),
        dma((4,)),
        dma((learners,)), dma((learners,)), dma((learners,)), dma((learners,)),
        dma((groups,)), dma((groups,)), dma((learners,)), dma((owners,)),
        dma((FLOW_STEPS, 2)), dma((FLOW_STEPS, 2)), dma((FLOW_STEPS, 2)), dma((FLOW_STEPS, 2)),
    ]
    return kernel, scratch


def store_kernel(field_ref, first_ref, second_ref, field_out, first_out, second_out, sem):
    copies = [
        pltpu.make_async_copy(
            field_ref.at[part], field_out.at[:, pl.ds(part * LANES, LANES)], sem.at[part])
        for part in range(2)
    ]
    copies.append(pltpu.make_async_copy(first_ref, first_out, sem.at[2]))
    copies.append(pltpu.make_async_copy(second_ref, second_out, sem.at[3]))
    for copy in copies:
        copy.start()
    for copy in copies:
        copy.wait()


def shards(field, first_weight, second_weight, face_edges, sample_index, route):
    points = field.shape[0]
    elements = field.shape[3]
    nodes = points**3
    width = first_weight.shape[1]
    learners = lax.axis_size("solver")
    groups = lax.axis_size("group")
    deriv, end_weight = gll_tables(points)
    gain = 2.0 / end_weight
    high, low = element_operator(deriv, gain)
    kernel, scratch = make_kernel(learners, groups, points, width, deriv, gain)
    vmem = pl.BlockSpec(memory_space=pltpu.VMEM)
    hbm = pl.BlockSpec(memory_space=pltpu.HBM)
    results = pl.pallas_call(
        kernel,
        out_shape=(
            jax.ShapeDtypeStruct((2, nodes, LANES), F32),
            jax.ShapeDtypeStruct(first_weight.shape, BF16),
            jax.ShapeDtypeStruct((1, width), BF16),
        ),
        in_specs=[hbm] + [vmem] * 5 + [hbm] * 2,
        out_specs=(vmem, vmem, vmem),
        scratch_shapes=scratch,
        compiler_params=pltpu.CompilerParams(
            collective_id=0, has_side_effects=True, vmem_limit_bytes=48 * 1024 * 1024
        ),
        name="step",
    )(
        field.reshape(nodes, elements),
        first_weight,
        second_weight.reshape(1, width),
        face_edges,
        sample_index.reshape(1, -1),
        route.reshape(1, -1),
        jnp.asarray(high),
        jnp.asarray(low),
    )
    new_field, new_first, new_second = pl.pallas_call(
        store_kernel,
        out_shape=(
            jax.ShapeDtypeStruct((nodes, elements), F32),
            jax.ShapeDtypeStruct(first_weight.shape, BF16),
            jax.ShapeDtypeStruct((1, width), BF16),
        ),
        in_specs=[vmem] * 3,
        out_specs=(hbm, hbm, hbm),
        scratch_shapes=[pltpu.SemaphoreType.DMA((4,))],
        name="store",
    )(*results)
    return (new_field.reshape(field.shape), new_first, new_second.reshape(second_weight.shape))


def solution(mesh):
    return jax.shard_map(
        shards,
        mesh=mesh,
        in_specs=(
            P(None, None, None, ("solver", "group")),
            P(),
            P(),
            P(),
            P(("solver", "group")),
            P(("solver", "group"), None),
        ),
        out_specs=(P(None, None, None, ("solver", "group")), P(), P()),
        check_vma=False,
    )
```

```python
import jax
import jax.numpy as jnp
import numpy as np
from jax import lax
from jax.experimental import pallas as pl
from jax.experimental.pallas import tpu as pltpu
from jax.sharding import PartitionSpec as P

FLOW_STEPS = 5
EXL = 4
EZL = 8
EY = 8

HIGH = lax.Precision.HIGHEST
TIME_STEP = 0.002
VISCOSITY = 0.01
VELOCITY = 1.0
PENALTY = 1.0
STRESS_SCALE = 0.1
LEARN_RATE = 0.05
LANES = 128
F32 = jnp.float32
BF16 = jnp.bfloat16


def legendre_table(points_x, points):
    table = np.zeros((points_x.shape[0], points))
    table[:, 0] = 1.0
    table[:, 1] = points_x
    for degree in range(2, points):
        table[:, degree] = (
            (2 * degree - 1) * points_x * table[:, degree - 1] - (degree - 1) * table[:, degree - 2]
        ) / degree
    return table


def gll_tables(points):
    order = points - 1
    guess = np.cos(np.pi * np.arange(points) / order)
    for sweep in range(100):
        table = legendre_table(guess, points)
        guess = guess - (guess * table[:, order] - table[:, order - 1]) / (points * table[:, order])
    nodes = guess[::-1]
    values = legendre_table(nodes, points)[:, order]
    matrix = np.zeros((points, points))
    for row in range(points):
        for column in range(points):
            if row != column:
                matrix[row, column] = values[row] / (values[column] * (nodes[row] - nodes[column]))
    matrix[0, 0] = -order * (order + 1) / 4.0
    matrix[order, order] = order * (order + 1) / 4.0
    return matrix.astype(np.float32), 2.0 / (order * (order + 1))


def element_operator(deriv, gain):
    points = deriv.shape[0]
    last = points - 1
    deriv = deriv.astype(np.float64)
    second = 4.0 * VISCOSITY * (deriv @ deriv)
    along_i = -2.0 * VELOCITY * deriv + second
    along_i[0, 0] -= gain * (VELOCITY + PENALTY)
    along_i[last, last] -= gain * PENALTY
    other = second.copy()
    other[0, 0] -= gain * PENALTY
    other[last, last] -= gain * PENALTY
    eye = np.eye(points)
    whole = (
        np.kron(np.kron(along_i, eye), eye)
        + np.kron(np.kron(eye, other), eye)
        + np.kron(np.kron(eye, eye), other)
    )
    whole = (TIME_STEP * whole).astype(np.float32)
    high = whole.astype(jnp.bfloat16)
    low = (whole - high.astype(np.float32)).astype(jnp.bfloat16)
    return high, low


def make_kernel(learners, groups, points, width, deriv, gain):
    face = points * points
    last = points - 1
    nodes = face * points
    walls = EXL * EZL
    elements = walls * EY
    pairs = walls * face // (2 * LANES)
    owners = min(learners, width // LANES)
    owned = width // owners
    devices = learners * groups
    block = EZL * EY
    half = LANES // 2
    step_gain = float(TIME_STEP * gain * PENALTY)
    step_gain_x = float(TIME_STEP * gain * (VELOCITY + PENALTY))
    first_row = [float(value) for value in deriv[0]]

    def roll(value, shift):
        shift = shift % LANES
        return value if shift == 0 else pltpu.roll(value, shift, 1)

    rows_sent = points + 1
    lane_rows = walls * face // LANES

    def kernel(
        field_ref, first_ref, second_ref, edges_ref, index_ref, route_ref, high_hbm, low_hbm,
        out_ref, new_first_ref, new_second_ref,
        u_ref, high_ref, low_ref, mask_ref, mixed_ref, feat_ref, turn_ref, z_ref, g_ref, e_ref,
        w2_ref, acc_ref, acc2_ref,
        count_ref, tile_ref, part_ref, cross_ref, total_ref, stress_ref,
        xs_ref, xr_ref, zs_ref, zr_ref,
        load_sem, count_send, count_recv, part_send, part_recv, cross_send, cross_recv,
        total_send, total_recv, xs_send, xr_recv, zs_send, zr_recv,
    ):
        me = lax.axis_index("solver")
        mine = lax.axis_index("group")

        def peer_s(offset):
            return lax.rem(me + offset, learners)

        def peer_g(offset):
            return lax.rem(mine + offset, groups)

        loads = [
            pltpu.make_async_copy(
                field_ref.at[:, pl.ds(part * LANES, LANES)], u_ref.at[0, part], load_sem.at[part])
            for part in range(2)
        ]
        loads.append(pltpu.make_async_copy(high_hbm, high_ref, load_sem.at[2]))
        loads.append(pltpu.make_async_copy(low_hbm, low_ref, load_sem.at[3]))
        for load in loads:
            load.start()

        barrier = pltpu.get_barrier_semaphore()
        for offset in range(1, learners):
            pl.semaphore_signal(
                barrier, inc=1, device_id={"solver": peer_s(offset)},
                device_id_type=pl.DeviceIdType.MESH,
            )
        for offset in range(1, groups):
            pl.semaphore_signal(
                barrier, inc=1, device_id={"group": peer_g(offset)},
                device_id_type=pl.DeviceIdType.MESH,
            )

        def remote(source, target, send, recv, where):
            return pltpu.make_async_remote_copy(
                src_ref=source, dst_ref=target, send_sem=send, recv_sem=recv,
                device_id=where, device_id_type=pl.DeviceIdType.MESH,
            )

        lane = lax.broadcasted_iota(jnp.int32, (1, LANES), 1)
        low_half = lane < half
        slot = lax.rem(lane, block) // EY
        level = lax.rem(lane, EY)
        contract = (((1,), (1,)), ((), ()))

        learner_rows = lax.broadcasted_iota(jnp.int32, (learners, route_ref.shape[1]), 0)
        hits = (route_ref[...] == learner_rows).astype(F32)
        count_ref[me] = jnp.broadcast_to(jnp.sum(hits, axis=1, keepdims=True), (learners, LANES))

        big = 2 * LANES
        edge_rows = lax.rem(
            lax.broadcasted_iota(jnp.int32, (big, edges_ref.shape[1]), 0), face)
        source = (edges_ref[0:1, :] == edge_rows).astype(F32).astype(BF16)
        sink = (edges_ref[1:2, :] == edge_rows).astype(F32).astype(BF16)
        node_rows = lax.broadcasted_iota(jnp.int32, (big, big), 0)
        node_cols = lax.broadcasted_iota(jnp.int32, (big, big), 1)
        graph = 0.25 * lax.dot_general(source, sink, contract, preferred_element_type=F32)
        graph = jnp.where(node_rows // face == node_cols // face, graph, 0.0)
        graph = graph + (node_rows == node_cols).astype(F32)
        small = graph[:LANES, :LANES]
        graph = graph.astype(BF16)
        first = first_ref[...].astype(F32)
        second = second_ref[...].astype(F32)

        def copies(step):
            right, left = {"solver": peer_s(1)}, {"solver": peer_s(learners - 1)}
            up, down = {"group": peer_g(1)}, {"group": peer_g(groups - 1)}
            result = []
            for side, where in ((0, right), (1, left)):
                result.append(remote(
                    xs_ref.at[step, side], xr_ref.at[step, side],
                    xs_send.at[step, side], xr_recv.at[step, side], where))
            for side, where in ((0, up), (1, down)):
                result.append(remote(
                    zs_ref.at[step, side], zr_ref.at[step, side],
                    zs_send.at[step, side], zr_recv.at[step, side], where))
            return result

        half_face = face // 2

        def near(i):
            return pl.ds(i * face, points, stride=points)

        def far(i):
            return pl.ds(i * face + last, points, stride=points)

        def send_z(step, bottoms, tops):
            for part in range(2):
                high_pack = jnp.zeros((points, LANES), F32)
                low_pack = jnp.zeros((points, LANES), F32)
                for i in range(points):
                    high_pack = jnp.where(slot == i, roll(tops[part][i], EY * (i + 1)), high_pack)
                    low_pack = jnp.where(slot == i, roll(bottoms[part][i], EY * i), low_pack)
                zs_ref[step, 0, part] = high_pack
                zs_ref[step, 1, part] = low_pack
            every = copies(step)
            every[2].start()
            every[3].start()

        def send_x(step, u):
            upper = u[1, pl.ds(nodes - face, face), :]
            xs_ref[step, 0] = jnp.where(low_half, roll(upper[:half_face], half), upper[half_face:])
            lower = u[0, pl.ds(0, face), :]
            xs_ref[step, 1] = jnp.where(low_half, lower[:half_face], roll(lower[half_face:], half))
            every = copies(step)
            every[0].start()
            every[1].start()

        def send_faces(step, u):
            send_z(step, [[u[part, near(i), :] for i in range(points)] for part in range(2)],
                   [[u[part, far(i), :] for i in range(points)] for part in range(2)])
            send_x(step, u)

        start = u_ref.at[0]
        for load in loads[:2]:
            load.wait()

        def face_rows(value_of):
            rows = jnp.concatenate([value_of(i) for i in range(points)], axis=0)
            return jnp.concatenate([rows, rows], axis=0).astype(BF16)

        def plane(i, j):
            at = pl.ds(i * face + j * points, points)
            return jnp.concatenate([start[0, at, :], start[1, at, :]], axis=1)

        def slope(i):
            total = None
            for j in range(points):
                term = first_row[j] * plane(i, j)
                total = term if total is None else total + term
            return STRESS_SCALE * total

        wall_rows = lax.broadcasted_iota(jnp.int32, (walls, elements), 0)
        wall_cols = lax.broadcasted_iota(jnp.int32, (walls, elements), 1)
        select = (wall_cols == wall_rows * EY).astype(F32).astype(BF16)
        for j in range(points):
            turn_ref[pl.ds(j * walls, walls), :] = lax.dot_general(
                select, face_rows(lambda i: plane(i, j)), contract, preferred_element_type=F32)
        turn_ref[pl.ds(points * walls, walls), :] = lax.dot_general(
            select, face_rows(slope), contract, preferred_element_type=F32)
        for row in range(lane_rows):
            even = turn_ref[pl.ds(2 * row, points, stride=walls), :]
            odd = turn_ref[pl.ds(2 * row + 1, points, stride=walls), :]
            feat_ref[row // 2, :, pl.ds((row % 2) * LANES, LANES)] = jnp.where(low_half, even, odd)
        target = jnp.where(
            low_half,
            turn_ref[pl.ds(points * walls, lane_rows, stride=2), :],
            turn_ref[pl.ds(points * walls + 1, lane_rows, stride=2), :],
        )

        pl.semaphore_wait(barrier, learners + groups - 2)
        for offset in range(1, learners):
            remote(count_ref.at[me], count_ref.at[me], count_send.at[offset], count_recv.at[me],
                   {"solver": peer_s(offset)}).start()
        send_faces(0, start)

        def network(first, second, learn):
            turned = jnp.transpose(first).astype(BF16)
            w2_ref[...] = jnp.transpose(jnp.broadcast_to(second, (LANES, width)))

            def one(pair, carry):
                before = jnp.dot(turned, feat_ref[pair].astype(BF16), preferred_element_type=F32)
                hidden = jnp.maximum(before, 0.0)
                if learn:
                    mask_ref[pair] = jnp.where(before > 0.0, 1.0, 0.0).astype(BF16)
                    mixed = jnp.dot(
                        hidden.astype(BF16), graph, preferred_element_type=F32).astype(BF16)
                    mixed_ref[pair] = mixed
                    hidden = mixed.astype(F32)
                weight = w2_ref[...]
                z_ref[pl.ds(2 * pair, 1), :] = jnp.sum(
                    hidden[:, :LANES] * weight, axis=0, keepdims=True)
                z_ref[pl.ds(2 * pair + 1, 1), :] = jnp.sum(
                    hidden[:, LANES:] * weight, axis=0, keepdims=True)
                return carry

            lax.fori_loop(0, pairs, one, 0)
            return z_ref[...]

        output = network(first, second, True)

        for offset in range(1, learners):
            origin = peer_s(offset)
            remote(count_ref.at[me], count_ref.at[origin], count_send.at[offset],
                   count_recv.at[origin], {"solver": origin}).wait_recv()
        counts = count_ref[0]
        for other in range(1, learners):
            counts = counts + count_ref[other]
        inverse = 1.0 / (jnp.maximum(counts, 1.0) * devices)
        places = 2 * lax.broadcasted_iota(jnp.int32, (lane_rows, index_ref.shape[1]), 0)
        chosen = (index_ref[...] == places).astype(F32)
        even = lax.dot_general(chosen, hits, contract, preferred_element_type=F32)
        chosen = (index_ref[...] == places + 1).astype(F32)
        odd = lax.dot_general(chosen, hits, contract, preferred_element_type=F32)
        difference = output - target
        error = jnp.zeros((lane_rows, LANES), F32)
        for learner in range(learners):
            times = jnp.where(low_half, even[:, learner:learner + 1], odd[:, learner:learner + 1])
            single = (difference * inverse[learner:learner + 1]).astype(BF16).astype(F32)
            error = error + times * single
        e_ref[...] = error
        g_ref[...] = lax.dot_general(
            error, small, contract, precision=HIGH, preferred_element_type=F32)

        acc_ref[...] = jnp.zeros_like(acc_ref)
        acc2_ref[...] = jnp.zeros_like(acc2_ref)

        def split(value):
            upper = value.astype(BF16).astype(F32)
            return jnp.concatenate([upper, value - upper], axis=0).astype(BF16)

        def row_pair(ref, pair):
            return jnp.concatenate([ref[pl.ds(2 * pair, 1), :], ref[pl.ds(2 * pair + 1, 1), :]], axis=1)

        def back(pair, carry):
            acc_ref[...] += lax.dot_general(
                split(feat_ref[pair] * row_pair(g_ref, pair)), mask_ref[pair], contract,
                preferred_element_type=F32)
            wide = jnp.broadcast_to(row_pair(e_ref, pair), (8, big))
            acc2_ref[...] += lax.dot_general(
                split(wide), mixed_ref[pair], contract, preferred_element_type=F32)
            return carry

        lax.fori_loop(0, pairs, back, 0)
        grad = acc_ref[0:points, :] + acc_ref[points:2 * points, :]
        grad_second = acc2_ref[0:1, :] + acc2_ref[8:9, :]
        for t in range(owners):
            tile_ref[t, pl.ds(0, points), :] = grad[:, t * owned:(t + 1) * owned]
            tile_ref[t, pl.ds(points, 1), :] = grad_second[:, t * owned:(t + 1) * owned]

        def when_owner(which, action):
            if owners == learners:
                action()
            else:
                pl.when(which < owners)(action)

        def clamp(which):
            return which if owners == learners else jnp.minimum(which, owners - 1)

        def part_copy(offset):
            where = peer_s(offset)
            return where, remote(tile_ref.at[clamp(where)], part_ref.at[me], part_send.at[offset],
                                 part_recv.at[me], {"solver": where})

        for offset in range(1, learners):
            where, copy = part_copy(offset)
            when_owner(where, copy.start)

        def local(source, target, stress):
            u = jnp.concatenate([source[0], source[1]], axis=1)
            upper = u.astype(BF16)
            lower = (u - upper.astype(F32)).astype(BF16)
            u = u + (
                jnp.dot(high_ref[...], upper, preferred_element_type=F32)
                + jnp.dot(high_ref[...], lower, preferred_element_type=F32)
                + jnp.dot(low_ref[...], upper, preferred_element_type=F32)
            )
            for part in range(2):
                target[part] = u[:, part * LANES:(part + 1) * LANES]
            for part in range(2):
                for i in range(points):
                    base = i * face
                    bottom = source[part, pl.ds(base, points), :]
                    top = source[part, pl.ds(base + face - points, points), :]
                    below = jnp.where(level == 0, bottom, roll(top, 1))
                    if stress:
                        below = below + stress_ref[part, pl.ds(i * points, points), :]
                    above = jnp.where(level == EY - 1, 0.0, roll(bottom, -1))
                    target[part, pl.ds(base, points), :] += step_gain * below
                    target[part, pl.ds(base + face - points, points), :] += step_gain * above
            low0 = roll(source[0, pl.ds(nodes - face, face), :], half)
            low1 = roll(source[1, pl.ds(nodes - face, face), :], half)
            target[0, pl.ds(0, face), :] += step_gain_x * jnp.where(low_half, 0.0, low0)
            target[1, pl.ds(0, face), :] += step_gain_x * jnp.where(low_half, low0, low1)
            high0 = roll(source[0, pl.ds(0, face), :], half)
            high1 = roll(source[1, pl.ds(0, face), :], half)
            target[0, pl.ds(nodes - face, face), :] += step_gain * jnp.where(low_half, high0, high1)
            target[1, pl.ds(nodes - face, face), :] += step_gain * jnp.where(low_half, high1, 0.0)
            for part in range(2):
                for i in range(points):
                    before = jnp.where(slot == 0, 0.0, roll(source[part, far(i), :], EY))
                    after = jnp.where(slot == EZL - 1, 0.0, roll(source[part, near(i), :], -EY))
                    target[part, near(i), :] = target[part, near(i), :] + step_gain * before
                    target[part, far(i), :] = target[part, far(i), :] + step_gain * after

        def halo(step, target, send):
            every = copies(step)
            every[0].wait_recv()
            every[1].wait_recv()
            ghost = xr_ref[step, 0]
            ghost = jnp.concatenate([ghost, roll(ghost, half)], axis=0)
            target[0, pl.ds(0, face), :] += step_gain_x * jnp.where(low_half, ghost, 0.0)
            ghost = xr_ref[step, 1]
            ghost = jnp.concatenate([roll(ghost, half), ghost], axis=0)
            target[1, pl.ds(nodes - face, face), :] += step_gain * jnp.where(low_half, 0.0, ghost)
            every[2].wait_recv()
            every[3].wait_recv()
            bottoms, tops = [], []
            for part in range(2):
                before_pack = step_gain * zr_ref[step, 0, part]
                after_pack = step_gain * zr_ref[step, 1, part]
                for i in range(points):
                    before = jnp.where(slot == 0, roll(before_pack, half - EY * i), 0.0)
                    after = jnp.where(
                        slot == EZL - 1, roll(after_pack, EY * (EZL - 1 - i)), 0.0)
                    bottoms.append(target[part, near(i), :] + before)
                    tops.append(target[part, far(i), :] + after)
                    target[part, near(i), :] = bottoms[-1]
                    target[part, far(i), :] = tops[-1]
            if send:
                send_z(step + 1, [bottoms[:points], bottoms[points:]], [tops[:points], tops[points:]])
                send_x(step + 1, target)

        for load in loads[2:]:
            load.wait()
        other = u_ref.at[1]
        local(start, other, False)
        halo(0, other, False)

        def reduce_owned():
            total = tile_ref[clamp(me)]
            for offset in range(1, learners):
                origin = peer_s(offset)
                remote(tile_ref.at[0], part_ref.at[origin], part_send.at[offset],
                       part_recv.at[origin], {"solver": origin}).wait_recv()
            for offset in range(1, learners):
                total = total + part_ref[peer_s(offset)]
            cross_ref[mine] = total
            for offset in range(1, groups):
                remote(cross_ref.at[mine], cross_ref.at[mine], cross_send.at[offset],
                       cross_recv.at[mine], {"group": peer_g(offset)}).start()
            for offset in range(1, groups):
                origin = peer_g(offset)
                remote(cross_ref.at[mine], cross_ref.at[origin], cross_send.at[offset],
                       cross_recv.at[origin], {"group": origin}).wait_recv()
            total = cross_ref[0]
            for origin in range(1, groups):
                total = total + cross_ref[origin]
            at = clamp(me)
            total_ref[at] = total
            for offset in range(1, learners):
                remote(total_ref.at[at], total_ref.at[at], total_send.at[offset],
                       total_recv.at[at], {"solver": peer_s(offset)}).start()

        when_owner(me, reduce_owned)
        for offset in range(1, learners):
            origin = peer_s(offset)
            at = clamp(origin)
            copy = remote(total_ref.at[at], total_ref.at[at], total_send.at[offset],
                          total_recv.at[at], {"solver": origin})
            when_owner(origin, copy.wait_recv)

        sums = jnp.concatenate([total_ref[t] for t in range(owners)], axis=1)
        grad = sums[0:points]
        new_first = (first - LEARN_RATE * (grad * second)).astype(BF16)
        new_second = (second - LEARN_RATE * sums[points:points + 1]).astype(BF16)
        new_first_ref[...] = new_first
        new_second_ref[...] = new_second

        plain = network(new_first.astype(F32), new_second.astype(F32), False)
        stress = jnp.dot(plain, small, precision=HIGH, preferred_element_type=F32)
        stress = jnp.transpose(stress)
        rows_t = 2 * lax.broadcasted_iota(jnp.int32, (lane_rows, elements), 0)
        cols_t = lax.broadcasted_iota(jnp.int32, (lane_rows, elements), 1)
        placed = jnp.dot(
            stress[:face], (cols_t == rows_t * EY).astype(F32),
            precision=HIGH, preferred_element_type=F32,
        ) + jnp.dot(
            stress[face:], (cols_t == (rows_t + 1) * EY).astype(F32),
            precision=HIGH, preferred_element_type=F32,
        )
        for part in range(2):
            columns = placed[:, part * LANES:(part + 1) * LANES]
            stress_ref[part] = columns
            for i in range(points):
                other[part, pl.ds(i * face, points), :] += (
                    step_gain * columns[i * points:(i + 1) * points])

        if FLOW_STEPS > 1:
            send_faces(1, other)
        held = [start, other]
        for step in range(1, FLOW_STEPS):
            final = step == FLOW_STEPS - 1
            source, target = held[step % 2], held[(step + 1) % 2]
            local(source, target, True)
            halo(step, target, not final)
        for part in range(2):
            out_ref[:, part * LANES:(part + 1) * LANES] = held[FLOW_STEPS % 2][part]

        for offset in range(1, learners):
            remote(count_ref.at[me], count_ref.at[me], count_send.at[offset], count_recv.at[me],
                   {"solver": peer_s(offset)}).wait_send()
            where, copy = part_copy(offset)
            when_owner(where, copy.wait_send)

        def drain_owned():
            at = clamp(me)
            for offset in range(1, groups):
                remote(cross_ref.at[mine], cross_ref.at[mine], cross_send.at[offset],
                       cross_recv.at[mine], {"group": peer_g(offset)}).wait_send()
            for offset in range(1, learners):
                remote(total_ref.at[at], total_ref.at[at], total_send.at[offset],
                       total_recv.at[at], {"solver": peer_s(offset)}).wait_send()

        when_owner(me, drain_owned)
        for step in range(FLOW_STEPS):
            for copy in copies(step):
                copy.wait_send()

    dma = pltpu.SemaphoreType.DMA
    scratch = [
        pltpu.VMEM((2, 2, nodes, LANES), F32),
        pltpu.VMEM((nodes, nodes), BF16),
        pltpu.VMEM((nodes, nodes), BF16),
        pltpu.VMEM((pairs, width, 2 * LANES), BF16),
        pltpu.VMEM((pairs, width, 2 * LANES), BF16),
        pltpu.VMEM((pairs, points, 2 * LANES), F32),
        pltpu.VMEM((points * walls + walls, LANES), F32),
        pltpu.VMEM((lane_rows, LANES), F32),
        pltpu.VMEM((lane_rows, LANES), F32),
        pltpu.VMEM((lane_rows, LANES), F32),
        pltpu.VMEM((width, LANES), F32),
        pltpu.VMEM((2 * points, width), F32),
        pltpu.VMEM((16, width), F32),
        pltpu.VMEM((learners, learners, LANES), F32),
        pltpu.VMEM((owners, rows_sent, owned), F32),
        pltpu.VMEM((learners, rows_sent, owned), F32),
        pltpu.VMEM((groups, rows_sent, owned), F32),
        pltpu.VMEM((owners, rows_sent, owned), F32),
        pltpu.VMEM((2, face, LANES), F32),
        pltpu.VMEM((FLOW_STEPS, 2, face // 2, LANES), F32),
        pltpu.VMEM((FLOW_STEPS, 2, face // 2, LANES), F32),
        pltpu.VMEM((FLOW_STEPS, 2, 2, points, LANES), F32),
        pltpu.VMEM((FLOW_STEPS, 2, 2, points, LANES), F32),
        dma((4,)),
        dma((learners,)), dma((learners,)), dma((learners,)), dma((learners,)),
        dma((groups,)), dma((groups,)), dma((learners,)), dma((owners,)),
        dma((FLOW_STEPS, 2)), dma((FLOW_STEPS, 2)), dma((FLOW_STEPS, 2)), dma((FLOW_STEPS, 2)),
    ]
    return kernel, scratch


def shards(field, first_weight, second_weight, face_edges, sample_index, route):
    points = field.shape[0]
    elements = field.shape[3]
    nodes = points**3
    width = first_weight.shape[1]
    learners = lax.axis_size("solver")
    groups = lax.axis_size("group")
    deriv, end_weight = gll_tables(points)
    gain = 2.0 / end_weight
    high, low = element_operator(deriv, gain)
    kernel, scratch = make_kernel(learners, groups, points, width, deriv, gain)
    vmem = pl.BlockSpec(memory_space=pltpu.VMEM)
    hbm = pl.BlockSpec(memory_space=pltpu.HBM)
    new_field, new_first, new_second = pl.pallas_call(
        kernel,
        out_shape=(
            jax.ShapeDtypeStruct((nodes, elements), F32),
            jax.ShapeDtypeStruct(first_weight.shape, BF16),
            jax.ShapeDtypeStruct((1, width), BF16),
        ),
        in_specs=[hbm] + [vmem] * 5 + [hbm] * 2,
        out_specs=(vmem, vmem, vmem),
        scratch_shapes=scratch,
        compiler_params=pltpu.CompilerParams(
            collective_id=0, has_side_effects=True, vmem_limit_bytes=67_043_328
        ),
        name="step",
    )(
        field.reshape(nodes, elements),
        first_weight,
        second_weight.reshape(1, width),
        face_edges,
        sample_index.reshape(1, -1),
        route.reshape(1, -1),
        jnp.asarray(high),
        jnp.asarray(low),
    )
    return (new_field.reshape(field.shape), new_first, new_second.reshape(second_weight.shape))


def solution(mesh):
    return jax.shard_map(
        shards,
        mesh=mesh,
        in_specs=(
            P(None, None, None, ("solver", "group")),
            P(),
            P(),
            P(),
            P(("solver", "group")),
            P(("solver", "group"), None),
        ),
        out_specs=(P(None, None, None, ("solver", "group")), P(), P()),
        check_vma=False,
    )
```
